32 devices in a mesh: dp: 8 (over z, x), tm: 4 (over y, core).
Axes of the slice: x: 2, y: 2, z: 4, core: 2. Of those that a mesh axis runs over, the one named last changes fastest.
Arguments:
- clips: bfloat16 [8, 32, 16, 16, 256], P('dp', 'tm'), may hold values from -6 to 6
- frame_counts: int32 [8], P('dp'), may hold values from 5 to 32, as said below
- weight: bfloat16 [6912, 256], P('dp'), may hold values from -0.078125 to 0.078125
- gain: float32 [256], replicated, may hold values from 0.1 to 1.9
- bias: float32 [256], replicated, may hold values from -3 to 3
- cotangent: bfloat16 [8, 16, 8, 8, 256], P('dp', 'tm'), may hold values from -6 to 6
Outputs:
- output: bfloat16 [8, 16, 8, 8, 256], P('dp', 'tm')
- input_grad: bfloat16 [8, 32, 16, 16, 256], P('dp', 'tm')
- weight_grad: float32 [6912, 256], P('dp')
The draws below stay inside these ranges and needn't reach their ends.
Inputs may be any that keep to these rules, and one draw needn't show every extreme that they name: frame_counts[c] frames of clip c are valid, the remaining slots are padding; in every draw some clip uses all 32 slots.
All inputs are finite; a program needn't handle non-finite values.
Results may differ from the reference program's by a relative error of at most 0.0048.
Values may be sent and summed in bfloat16 or wider, within the bound.
A program may use at most 64 MiB of HBM per device.

```python
import jax
import jax.numpy as jnp
from jax import lax

CHANNELS = 256
GROUPS = 32
ROWS = 16
COLS = 16
CLIPS = 8
FRAMES = 32


def draw_frame_counts(key, part):
    first_key = jax.random.fold_in(key, 11)
    second_key = jax.random.fold_in(key, 12)
    counts = jax.random.randint(first_key, (CLIPS,), FRAMES // 8 + 1, FRAMES + 1)
    position = jax.random.randint(second_key, (), 0, CLIPS)
    return jnp.where(jnp.arange(CLIPS) == position, FRAMES, counts).astype(jnp.int32)


def steps_of(rng, dims, shards, smallest, top_value):
    factor_of, own = 1.0, jax.random.fold_in(rng, 6)
    for axis_at, parts in shards:
        heights = jnp.exp(jax.random.uniform(jax.random.fold_in(own, axis_at), (parts,), jnp.float32, smallest / len(shards), top_value / len(shards)))
        factor_of = factor_of * jnp.repeat(heights, dims[axis_at] // parts).reshape([-1 if axis == axis_at else 1 for axis in range(len(dims))])
    return factor_of


def centred(rng, shape, spread, bound, cuts=(), dtype=jnp.bfloat16):
    array = jax.random.normal(rng, shape, jnp.float32) * spread
    if len(cuts) > 0:
        array = steps_of(rng, shape, cuts, -0.22, 0.18) * array
    return jnp.clip(array, min=-bound, max=bound).astype(dtype)


def setup_inputs(seed: int = 0) -> dict:
    seeds = jax.random.split(jax.random.key(seed), 7)
    clips = centred(seeds[0], (CLIPS, FRAMES, ROWS, COLS, CHANNELS), 1.0, 6.0, ((0, 8), (1, 4)))
    frame_counts = draw_frame_counts(jax.random.fold_in(seeds[6], 71), 0)
    weight = centred(seeds[2], (27 * CHANNELS, CHANNELS), (27 * CHANNELS) ** -0.5, 0.078125, ((0, 8),))
    gain = jnp.clip(1.0 + 0.18 * jax.random.normal(seeds[3], (CHANNELS,), jnp.float32), 0.1, 1.9)
    bias = centred(seeds[4], (CHANNELS,), 0.5, 3.0, (), jnp.float32)
    cotangent = centred(seeds[5], (CLIPS, FRAMES // 2, ROWS // 2, COLS // 2, CHANNELS), 1.0, 6.0, ((0, 8), (1, 4)))
    return dict(clips=clips, frame_counts=frame_counts, weight=weight, gain=gain, bias=bias, cotangent=cotangent)


EPS = 1e-06

def unfold(padded, frames_out, rows_out, cols_out):
    tap_list = []
    for step_t in range(3):
        for step_r in range(3):
            for step_c in range(3):
                tap_piece = padded[step_t:step_t + 2 * frames_out:2, step_r:step_r + 2 * rows_out:2, step_c:step_c + 2 * cols_out:2, :]
                tap_list.append(tap_piece.reshape(frames_out * rows_out * cols_out, -1))
    return jnp.concatenate(tap_list, axis=1)

def spread_taps(values, data_axis, tap_axis, length):
    moved = jnp.moveaxis(values, tap_axis, 0)
    count = moved.shape[data_axis + 1]
    width_list = [(0, 0)] * (moved.ndim - 1)
    after = list(width_list)
    after[data_axis] = (0, 1)
    before = list(width_list)
    before[data_axis] = (1, 0)
    even_part = jnp.pad(moved[0], after) + jnp.pad(moved[2], before)
    odd_part = jnp.pad(moved[1], after)
    joined = jnp.stack([even_part, odd_part], axis=data_axis + 1)
    shape_new = list(even_part.shape)
    shape_new[data_axis] = 2 * (count + 1)
    joined = joined.reshape(shape_new)
    return lax.slice_in_dim(joined, 0, length, axis=data_axis)

def fold_back(columns, padded_shape, frames_out, rows_out, cols_out):
    channels = padded_shape[3]
    blocks = columns.reshape(frames_out, rows_out, cols_out, 3, 3, 3, channels)
    blocks = spread_taps(blocks, 0, 3, padded_shape[0])
    blocks = spread_taps(blocks, 1, 3, padded_shape[1])
    blocks = spread_taps(blocks, 2, 3, padded_shape[2])
    return blocks

def silu_slope(preact):
    sig = jax.nn.sigmoid(preact)
    return sig * (1.0 + preact * (1.0 - sig))

def reference(clips, frame_counts, weight, gain, bias, cotangent):

    def clip_pass(running, scanned):
        clip_data, frames_valid, cot_block = scanned
        frame_count, row_count, col_count, channels = clip_data.shape
        width_g = channels // GROUPS
        frame_mask = (jnp.arange(frame_count) < frames_valid).astype(jnp.float32)[:, None, None, None]
        mask_group = frame_mask[..., None]
        entries = frames_valid.astype(jnp.float32) * (row_count * col_count * width_g)
        values = clip_data.astype(jnp.float32).reshape(frame_count, row_count, col_count, GROUPS, width_g)
        sum_first = lax.optimization_barrier(jnp.sum(values * mask_group, axis=(0, 1, 2, 4)))
        sum_second = lax.optimization_barrier(jnp.sum(values * values * mask_group, axis=(0, 1, 2, 4)))
        group_mean = sum_first / entries
        variance = sum_second / entries - group_mean * group_mean
        inv_std = lax.rsqrt(variance + EPS)
        normed_g = (values - group_mean[:, None]) * inv_std[:, None]
        normed = normed_g.reshape(frame_count, row_count, col_count, channels)
        preact = normed * gain + bias
        hidden = (jax.nn.silu(preact) * frame_mask).astype(jnp.bfloat16)
        padded = jnp.pad(hidden, ((2, 0), (1, 0), (1, 0), (0, 0)))
        frames_out, rows_out, cols_out = (frame_count // 2, row_count // 2, col_count // 2)
        patches = unfold(padded, frames_out, rows_out, cols_out)
        out_block = jnp.dot(patches, weight, preferred_element_type=jnp.float32).astype(jnp.bfloat16)
        out_block = out_block.reshape(frames_out, rows_out, cols_out, channels)
        cot_rows = cot_block.reshape(-1, channels)
        weight_grad = running + lax.dot_general(patches, cot_rows, (((0,), (0,)), ((), ())), preferred_element_type=jnp.float32)
        dcols = lax.dot_general(cot_rows, weight, (((1,), (1,)), ((), ())), preferred_element_type=jnp.float32)
        dpad = fold_back(dcols, padded.shape, frames_out, rows_out, cols_out)
        dhidden = dpad[2:, 1:, 1:, :]
        dnormed = dhidden * frame_mask * silu_slope(preact) * gain
        grad_norm = dnormed.reshape(frame_count, row_count, col_count, GROUPS, width_g)
        back_first = lax.optimization_barrier(jnp.sum(grad_norm, axis=(0, 1, 2, 4)))
        back_second = lax.optimization_barrier(jnp.sum(grad_norm * normed_g, axis=(0, 1, 2, 4)))
        input_grad = mask_group * inv_std[:, None] * (grad_norm - back_first[:, None] / entries - normed_g * back_second[:, None] / entries)
        input_grad = input_grad.reshape(frame_count, row_count, col_count, channels).astype(jnp.bfloat16)
        return (weight_grad, (out_block, input_grad))
    start_grad = jnp.zeros(weight.shape, jnp.float32)
    weight_grad, (output, input_grad) = lax.scan(clip_pass, start_grad, (clips, frame_counts, cotangent))
    return (output, input_grad, weight_grad)
```

```python
import functools

import jax
import jax.numpy as jnp
from jax import lax
from jax.experimental import pallas as pl
from jax.experimental.pallas import tpu as pltpu
from jax.sharding import PartitionSpec as P

GROUPS = 32
EPS = 1e-06
PARTS = 3
MESH = pl.DeviceIdType.MESH
VMEM = pl.BlockSpec(memory_space=pltpu.VMEM)
SMEM = pl.BlockSpec(memory_space=pltpu.SMEM)


def shifted(value, axis, by):
    devices = lax.axis_size(axis)
    pairs = [(i, i + by) for i in range(devices) if 0 <= i + by < devices]
    return lax.ppermute(value, axis, pairs)


def forward_kernel(place_ref, params_ref, earlier_ref, clip_ref, cot_ref, patch_ref, grad_ref, held):
    frames, half_rows, _, cols, channels = clip_ref.shape
    half_cols, lanes = cols // 2, channels // 128
    area = half_rows * half_cols
    first, valid = place_ref[0], place_ref[1]
    mean, inv_std = params_ref[0:1, :], params_ref[1:2, :]
    gain, bias = params_ref[2:3, :], params_ref[3:4, :]
    held[...] = jnp.zeros_like(held)
    for frame in range(frames + 1):
        source = earlier_ref.at[frame] if frame < 2 else clip_ref.at[frame - 2]
        slot = first + (frame - 2)
        mask = jnp.where((slot >= 0) & (slot < valid), 1.0, 0.0).astype(jnp.float32)

        def rows(index, _):
            values = source[index].astype(jnp.float32)
            preact = (values - mean) * inv_std * gain + bias
            hidden = preact / (1.0 + jnp.exp(-preact)) * mask
            for lane in range(lanes):
                part = hidden[:, :, lane * 128 : (lane + 1) * 128]
                held[lane, index, 1, 8 : 8 + cols, :] = part[0]
                held[lane, index + 1, 0, 8 : 8 + cols, :] = part[1]
            return 0

        lax.fori_loop(0, half_rows, rows, 0, unroll=2)
        for step_r in range(3):
            for step_c in range(3):
                pieces = [
                    held[
                        lane,
                        step_r // 2 : step_r // 2 + half_rows,
                        step_r % 2,
                        pl.ds(7 + step_c, half_cols, 2),
                        :,
                    ].reshape(area, 128)
                    for lane in range(lanes)
                ]
                piece = jnp.concatenate(pieces, axis=1).astype(jnp.bfloat16)
                for step_t in range(3):
                    if (frame - step_t) % 2 == 0 and 0 <= frame - step_t < frames:
                        place = (frame - step_t) // 2
                        tap = 9 * step_t + 3 * step_r + step_c
                        patch_ref[
                            place * area : (place + 1) * area,
                            tap * channels : (tap + 1) * channels,
                        ] = piece

    def tap_grad(tap, _):
        at = pl.multiple_of(tap * channels, channels)
        grad_ref[pl.ds(at, channels), :] = lax.dot_general(
            patch_ref[:, pl.ds(at, channels)],
            cot_ref[...],
            (((0,), (0,)), ((), ())),
            preferred_element_type=jnp.float32,
        )
        return 0

    lax.fori_loop(0, 27, tap_grad, 0)


def backward_kernel(
    place_ref, params_ref, patch_ref, weight_ref, cot_ref, clip_ref, out_ref, grad_ref, sums_ref, wide, views, spread
):
    frames, half_rows, _, cols, channels = clip_ref.shape
    frames_out, half_cols, lanes = frames // 2, cols // 2, channels // 128
    count = frames_out * half_rows * half_cols
    first, valid = place_ref[0], place_ref[1]
    mean, inv_std = params_ref[0:1, :], params_ref[1:2, :]
    gain, bias = params_ref[2:3, :], params_ref[3:4, :]
    total = jnp.zeros((count, channels), jnp.float32)
    depth = 9 * channels
    for step in range(3):
        total += jnp.dot(
            patch_ref[:, step * depth : (step + 1) * depth],
            weight_ref[step * depth : (step + 1) * depth, :],
            preferred_element_type=jnp.float32,
        )
    out_ref[...] = total.astype(jnp.bfloat16)
    wide[...] = jnp.zeros_like(wide)
    for frame in range(frames_out + 1):
        wide[frame, 0:half_rows, 0:half_cols, :] = cot_ref[frame].astype(jnp.float32)
    for dt in range(2):
        for dr in range(2):
            for dc in range(2):
                piece = wide[dt : dt + frames_out, dr : dr + half_rows, dc : dc + half_cols, :]
                views[4 * dt + 2 * dr + dc] = piece.reshape(count, channels).astype(jnp.bfloat16)
    times = (((2, 0), (0, 1)), ((1, 1),))
    spaces = (((1, 0),), ((2, 0), (0, 1)))
    for part_t in range(2):
        for part_r in range(2):
            for part_c in range(2):
                total = jnp.zeros((count, channels), jnp.float32)
                for step_t, dt in times[part_t]:
                    for step_r, dr in spaces[part_r]:
                        for step_c, dc in spaces[part_c]:
                            tap = 9 * step_t + 3 * step_r + step_c
                            total += lax.dot_general(
                                views[4 * dt + 2 * dr + dc],
                                weight_ref[tap * channels : (tap + 1) * channels, :],
                                (((1,), (1,)), ((), ())),
                                preferred_element_type=jnp.float32,
                            )
                total = total.reshape(frames_out, half_rows, half_cols, channels)
                for frame in range(frames_out):
                    for lane in range(lanes):
                        spread[
                            lane, 2 * frame + part_t, :, part_r, pl.ds(part_c, half_cols, 2), :
                        ] = total[frame, :, :, lane * 128 : (lane + 1) * 128]

    def rows(index, sums):
        frame, row = index // half_rows, index % half_rows
        mask = jnp.where(first + frame < valid, 1.0, 0.0).astype(jnp.float32)
        normed = (clip_ref[frame, row].astype(jnp.float32) - mean) * inv_std
        preact = normed * gain + bias
        sig = 1.0 / (1.0 + jnp.exp(-preact))
        slope = sig * (1.0 + preact * (1.0 - sig))
        hidden_grad = jnp.concatenate([spread[lane, frame, row] for lane in range(lanes)], axis=-1)
        value = hidden_grad * mask * slope * gain
        grad_ref[frame, row] = value
        return (
            sums[0] + jnp.sum(value.reshape(-1, 8, channels), axis=0),
            sums[1] + jnp.sum((value * normed).reshape(-1, 8, channels), axis=0),
        )

    zero = jnp.zeros((8, channels), jnp.float32)
    sums = lax.fori_loop(0, frames * half_rows, rows, (zero, zero), unroll=2)
    sums_ref[0] = sums[0]
    sums_ref[1] = sums[1]


def plan(dp_size, tm_size):
    dp_bits = [("dp", k) for k in range(dp_size.bit_length() - 1)]
    tm_bits = [("tm", k) for k in range(tm_size.bit_length() - 1)]
    cut = len(dp_bits) // 2
    ways = [tm_bits[1:], dp_bits[:cut], dp_bits[cut:]]
    orders = []
    for part in range(PARTS):
        turned = ways[part:] + ways[:part]
        orders.append(tm_bits[:1] + turned[0] + turned[1] + turned[2])
    return dp_bits[::-1] + tm_bits[::-1], orders


def reduce_kernel(labels, orders, grad_ref, out_ref, *scratch):
    depth = len(labels)
    sends, receives, kept = (scratch[i * depth : (i + 1) * depth] for i in range(3))
    send_sem, recv_sem, share_send, share_recv = scratch[3 * depth :]
    place = {"dp": lax.axis_index("dp"), "tm": lax.axis_index("tm")}

    def bit_of(label):
        return (place[label[0]] // 2 ** label[1]) % 2

    def partner(label):
        return {label[0]: place[label[0]] + (1 - 2 * bit_of(label)) * 2 ** label[1]}

    barrier = pltpu.get_barrier_semaphore()
    for label in labels:
        pl.semaphore_signal(barrier, inc=1, device_id=partner(label), device_id_type=MESH)
    pl.semaphore_wait(barrier, depth)

    left = [list(labels) for _ in range(PARTS)]
    copies = [[None] * depth for _ in range(PARTS)]

    def index_of(stride, number, bit):
        return (number // stride) * (2 * stride) + bit * stride + number % stride

    def read(stage, part, index):
        return grad_ref[index, part] if stage == 0 else kept[stage - 1][part, index]

    def add(stage, part):
        label = orders[part][stage]
        stride = 2 ** (len(left[part]) - 1 - left[part].index(label))
        number = 2 ** (len(left[part]) - 1)
        copies[part][stage].wait_recv()

        def one(block, _):
            kept[stage][part, block] = read(
                stage, part, index_of(stride, block, bit_of(label))
            ) + receives[stage][part, block].astype(jnp.float32)
            return 0

        lax.fori_loop(0, number, one, 0)
        left[part].remove(label)

    for stage in range(depth):
        for part in range(PARTS):
            if stage > 0:
                add(stage - 1, part)
            label = orders[part][stage]
            stride = 2 ** (len(left[part]) - 1 - left[part].index(label))
            number = 2 ** (len(left[part]) - 1)

            def pack(block, _):
                sends[stage][part, block] = read(
                    stage, part, index_of(stride, block, 1 - bit_of(label))
                ).astype(jnp.bfloat16)
                return 0

            lax.fori_loop(0, number, pack, 0)
            copies[part][stage] = pltpu.make_async_remote_copy(
                src_ref=sends[stage].at[part],
                dst_ref=receives[stage].at[part],
                send_sem=send_sem.at[part, stage],
                recv_sem=recv_sem.at[part, stage],
                device_id=partner(label),
                device_id_type=MESH,
            )
            copies[part][stage].start()
    own = place["tm"]
    for part in range(PARTS):
        add(depth - 1, part)
        out_ref[own, part] = kept[depth - 1][part, 0]

    tm_bits = [label for label in labels if label[0] == "tm"]
    shares, serial = [], 0
    for label in tm_bits:
        span = 2 ** (label[1] + 1)
        stage_shares = []
        for high in range(out_ref.shape[0] // span):
            block = high * span + own % span
            share = pltpu.make_async_remote_copy(
                src_ref=out_ref.at[block],
                dst_ref=out_ref.at[block],
                send_sem=share_send.at[serial],
                recv_sem=share_recv.at[serial],
                device_id=partner(label),
                device_id_type=MESH,
            )
            share.start()
            stage_shares.append(share)
            serial += 1
        for share in stage_shares:
            share.wait_recv()
        shares += stage_shares
    for share in shares:
        share.wait_send()
    for part in range(PARTS):
        for copy in copies[part]:
            copy.wait_send()


def reduce_grads(grads, dp_size, tm_size):
    labels, orders = plan(dp_size, tm_size)
    depth = len(labels)
    rows, channels = grads.shape
    devices = dp_size * tm_size
    piece = rows // (devices * PARTS)
    halves = [2 ** (depth - 1 - stage) for stage in range(depth)]
    half_shapes = [(PARTS, half, piece, channels) for half in halves]
    reduced = pl.pallas_call(
        functools.partial(reduce_kernel, labels, orders),
        out_shape=jax.ShapeDtypeStruct((tm_size, PARTS, piece, channels), jnp.float32),
        in_specs=[VMEM],
        out_specs=VMEM,
        scratch_shapes=[pltpu.VMEM(shape, jnp.bfloat16) for shape in half_shapes] * 2
        + [pltpu.VMEM(shape, jnp.float32) for shape in half_shapes]
        + [pltpu.SemaphoreType.DMA((PARTS, depth))] * 2
        + [pltpu.SemaphoreType.DMA((tm_size,))] * 2,
        compiler_params=pltpu.CompilerParams(
            collective_id=0, has_side_effects=True, vmem_limit_bytes=48 * 2**20
        ),
    )(grads.reshape(devices, PARTS, piece, channels))
    return reduced.reshape(rows // dp_size, channels)


def shards(dp_size, tm_size, clips, frame_counts, weight, gain, bias, cotangent):
    clip_data = clips[0]
    cot_block = cotangent[0]
    frame_count, row_count, col_count, channels = clip_data.shape
    frames_out, rows_out, cols_out = cot_block.shape[:3]
    count = frames_out * rows_out * cols_out
    width_g = channels // GROUPS
    first_frame = lax.axis_index("tm") * frame_count
    full_weight = lax.all_gather(weight, "dp", axis=0, tiled=True)
    split = (frame_count, row_count // 2, 2, col_count, channels)
    earlier = shifted(clip_data[-2:], "tm", 1).reshape((2,) + split[1:])
    cot_next = shifted(cot_block[:1], "tm", -1)
    frame_mask = (first_frame + jnp.arange(frame_count) < frame_counts[0]).astype(jnp.float32)[
        :, None, None, None
    ]
    entries = frame_counts[0].astype(jnp.float32) * (row_count * col_count * width_g)
    values = clip_data.astype(jnp.float32)
    held = values * frame_mask
    sums = jnp.stack([jnp.sum(held, axis=(0, 1, 2)), jnp.sum(held * values, axis=(0, 1, 2))])
    sums = lax.psum(jnp.sum(sums.reshape(2, GROUPS, width_g), axis=2), "tm")
    group_mean = sums[0] / entries
    variance = sums[1] / entries - group_mean * group_mean
    inv_std = lax.rsqrt(variance + EPS)
    mean_c = jnp.repeat(group_mean, width_g)
    inv_c = jnp.repeat(inv_std, width_g)
    params = jnp.concatenate([jnp.stack([mean_c, inv_c, gain, bias]), jnp.zeros((4, channels), jnp.float32)])
    place = jnp.stack([first_frame.astype(jnp.int32), frame_counts[0]])
    limit = pltpu.CompilerParams(vmem_limit_bytes=48 * 2**20)
    clip_split = clip_data.reshape(split)
    patches, grads = pl.pallas_call(
        forward_kernel,
        out_shape=(
            jax.ShapeDtypeStruct((count, 27 * channels), jnp.bfloat16),
            jax.ShapeDtypeStruct((27 * channels, channels), jnp.float32),
        ),
        in_specs=[SMEM] + [VMEM] * 4,
        out_specs=(VMEM, VMEM),
        scratch_shapes=[pltpu.VMEM((channels // 128, rows_out + 1, 2, col_count + 8, 128), jnp.float32)],
        compiler_params=limit,
    )(place, params, earlier, clip_split, cot_block.reshape(count, channels))
    weight_grad = reduce_grads(grads, dp_size, tm_size)
    output, dnormed, back = pl.pallas_call(
        backward_kernel,
        out_shape=(
            jax.ShapeDtypeStruct((count, channels), jnp.bfloat16),
            jax.ShapeDtypeStruct(split, jnp.float32),
            jax.ShapeDtypeStruct((2, 8, channels), jnp.float32),
        ),
        in_specs=[SMEM] + [VMEM] * 5,
        out_specs=(VMEM, VMEM, VMEM),
        scratch_shapes=[
            pltpu.VMEM((frames_out + 1, rows_out + 1, 16, channels), jnp.float32),
            pltpu.VMEM((8, count, channels), jnp.bfloat16),
            pltpu.VMEM((channels // 128,) + split[:-1] + (128,), jnp.float32),
        ],
        compiler_params=limit,
    )(place, params, patches, full_weight, jnp.concatenate([cot_block, cot_next]), clip_split)
    back = jnp.sum(back, axis=1).reshape(2, GROUPS, width_g)
    back = lax.psum(jnp.sum(back, axis=2), "tm") / entries
    first_c, second_c = jnp.repeat(back[0], width_g), jnp.repeat(back[1], width_g)
    normed = (values - mean_c) * inv_c
    dnormed = dnormed.reshape(clip_data.shape)
    input_grad = (frame_mask * inv_c * (dnormed - first_c - normed * second_c)).astype(jnp.bfloat16)
    return (output.reshape(cot_block.shape)[None], input_grad[None], weight_grad)


def solution(mesh):
    placed = (
        P("dp", "tm", None, None, None),
        P("dp"),
        P("dp", None),
        P(),
        P(),
        P("dp", "tm", None, None, None),
    )
    return jax.shard_map(
        functools.partial(shards, mesh.shape["dp"], mesh.shape["tm"]),
        mesh=mesh,
        in_specs=placed,
        out_specs=(P("dp", "tm", None, None, None), P("dp", "tm", None, None, None), P("dp", None)),
        check_vma=False,
    )
```

```python
import functools

import jax
import jax.numpy as jnp
from jax import lax
from jax.experimental import pallas as pl
from jax.experimental.pallas import tpu as pltpu
from jax.sharding import PartitionSpec as P

GROUPS = 32
EPS = 1e-06
PARTS = 3
MESH = pl.DeviceIdType.MESH
VMEM = pl.BlockSpec(memory_space=pltpu.VMEM)
SMEM = pl.BlockSpec(memory_space=pltpu.SMEM)


def plan(dp_size, tm_size):
    dp_bits = [("dp", k) for k in range(dp_size.bit_length() - 1)]
    tm_bits = [("tm", k) for k in range(tm_size.bit_length() - 1)]
    cut = len(dp_bits) // 2
    ways = [tm_bits[1:], dp_bits[:cut], dp_bits[cut:]]
    orders = []
    for part in range(PARTS):
        turned = ways[part:] + ways[:part]
        orders.append(tm_bits[:1] + turned[0] + turned[1] + turned[2])
    return dp_bits[::-1] + tm_bits[::-1], orders


def lane_group_sum(value, width):
    channels = value.shape[-1]
    lane = lax.broadcasted_iota(jnp.int32, value.shape, value.ndim - 1)
    step = 1
    while step < width:
        above = pltpu.roll(value, channels - step, value.ndim - 1)
        below = pltpu.roll(value, step, value.ndim - 1)
        value = value + jnp.where((lane // step) % 2 == 0, above, below)
        step *= 2
    return value


def block_kernel(
    labels, orders, dp_size, tm_size, near, width_g,
    valid_ref, params_ref, clip_ref, cot_ref, weight_ref,
    out_ref, input_grad_ref, weight_grad_ref,
    earlier, next_cot, full_weight, patches, grads, held, wide, views, spread, moments, sums_in, back_in,
    *scratch,
):
    frames, half_rows, _, cols, channels = clip_ref.shape
    frames_out, half_cols, lanes = frames // 2, cols // 2, channels // 128
    area = half_rows * half_cols
    count = frames_out * area
    depth = len(labels)
    sends, receives, kept = (scratch[i * depth : (i + 1) * depth] for i in range(3))
    (send_sem, recv_sem, share_send, share_recv, ring_send, ring_recv, sum_send, sum_recv,
     far_send, far_recv, near_send, near_recv, mate_send, mate_recv, own_sem) = scratch[3 * depth :]
    dp, tm = lax.axis_index("dp"), lax.axis_index("tm")
    place = {"dp": dp, "tm": tm}
    far_size = dp_size // near
    far_at, near_at = dp // near, dp % near
    core = tm % 2
    mate = {"tm": tm + 1 - 2 * core}

    def bit_of(label):
        return (place[label[0]] // 2 ** label[1]) % 2

    def partner(label):
        return {label[0]: place[label[0]] + (1 - 2 * bit_of(label)) * 2 ** label[1]}

    def send(source, target, sem_out, sem_in, device):
        copy = pltpu.make_async_remote_copy(
            src_ref=source, dst_ref=target, send_sem=sem_out, recv_sem=sem_in,
            device_id=device, device_id_type=MESH,
        )
        copy.start()
        return copy

    barrier = pltpu.get_barrier_semaphore()
    greeted = [{"tm": (tm + step) % tm_size} for step in range(1, tm_size)]
    greeted += [{"dp": dp_index} for dp_index in dp_peers(dp, dp_size, near)]
    for device in greeted:
        pl.semaphore_signal(barrier, inc=1, device_id=device, device_id_type=MESH)
    pl.semaphore_wait(barrier, len(greeted))

    ring = [
        send(clip_ref.at[frames - 2 : frames], earlier, ring_send.at[0], ring_recv.at[0], {"tm": (tm + 1) % tm_size}),
        send(cot_ref.at[0:area], next_cot, ring_send.at[1], ring_recv.at[1], {"tm": (tm + tm_size - 1) % tm_size}),
    ]

    rows_w = weight_ref.shape[0]
    half_lane = pl.ds(pl.multiple_of(core * 128, 128), 128)

    def block_at(index):
        return full_weight.at[pl.ds(pl.multiple_of(index * rows_w, 8), rows_w), half_lane]

    own_copy = pltpu.make_async_copy(
        weight_ref, full_weight.at[pl.ds(pl.multiple_of(dp * rows_w, 8), rows_w), :], own_sem
    )
    own_copy.start()
    own_half = weight_ref.at[:, half_lane]
    far_copies = [
        send(own_half, block_at(dp), far_send.at[step], far_recv.at[step],
             {"dp": ((far_at + step) % far_size) * near + near_at})
        for step in range(1, far_size)
    ]
    near_copies, mate_copies = {}, []

    def send_near(step, source, index):
        for hop in range(1, near):
            near_copies[step, hop] = send(
                source, block_at(index), near_send.at[step, hop], near_recv.at[step, hop],
                {"dp": far_at * near + (near_at + hop) % near},
            )

    def send_mate(step, hop, index):
        mate_copies.append(
            send(block_at(index), block_at(index), mate_send.at[step, hop], mate_recv.at[step, hop], mate)
        )

    send_near(0, own_half, dp)

    def weight_far(step):
        far_copies[step - 1].wait_recv()
        index = ((far_at + far_size - step) % far_size) * near + near_at
        send_near(step, block_at(index), index)
        send_mate(step, 0, index)

    def weight_near(step):
        for hop in range(1, near):
            near_copies[step, hop].wait_recv()
            index = ((far_at + far_size - step) % far_size) * near + (near_at + near - hop) % near
            send_mate(step, hop, index)

    first = tm * frames
    valid = valid_ref[0]
    gain, bias = params_ref[0:1, :], params_ref[1:2, :]
    entries = jnp.full((1, channels), valid.astype(jnp.float32)) * float(2 * half_rows * cols * width_g)
    zero = jnp.zeros((8, channels), jnp.float32)

    def fold(value):
        return jnp.sum(value.reshape(-1, 8, channels), axis=0)

    def frame_mask(frame):
        slot = first + frame
        return jnp.where((slot >= 0) & (slot < valid), 1.0, 0.0).astype(jnp.float32)

    def moment_rows(index, sums):
        frame, row = index // half_rows, index % half_rows
        values = clip_ref[frame, row].astype(jnp.float32)
        masked = values * frame_mask(frame)
        return sums[0] + fold(masked), sums[1] + fold(masked * values)

    def exchange(sums, buffer, sems):
        pair = [jnp.sum(value, axis=0, keepdims=True) for value in sums]
        buffer[tm] = jnp.concatenate(pair + [jnp.zeros((6, channels), jnp.float32)], axis=0)
        copies = [
            send(buffer.at[tm], buffer.at[tm], sum_send.at[sems, step], sum_recv.at[sems, step],
                 {"tm": (tm + step) % tm_size})
            for step in range(1, tm_size)
        ]

        def finish():
            for copy in copies:
                copy.wait()
            total = buffer[0]
            for index in range(1, tm_size):
                total = total + buffer[index]
            return lane_group_sum(total, width_g)

        return finish

    finish = exchange(lax.fori_loop(0, frames * half_rows, moment_rows, (zero, zero), unroll=2), sums_in, 0)
    held[...] = jnp.zeros_like(held)
    total = finish()
    mean = total[0:1] / entries
    inv_std = lax.rsqrt(total[1:2] / entries - mean * mean + EPS)
    for copy in ring:
        copy.wait()

    ticks = [functools.partial(weight_far, step) for step in range(1, far_size)]
    for frame in range(frames + 1):
        source = earlier.at[frame] if frame < 2 else clip_ref.at[frame - 2]
        mask = frame_mask(frame - 2)

        def rows(index, _):
            values = source[index].astype(jnp.float32)
            preact = (values - mean) * inv_std * gain + bias
            hidden = preact / (1.0 + jnp.exp(-preact)) * mask
            for lane in range(lanes):
                part = hidden[:, :, lane * 128 : (lane + 1) * 128]
                held[lane, index, 1, 8 : 8 + cols, :] = part[0]
                held[lane, index + 1, 0, 8 : 8 + cols, :] = part[1]
            return 0

        lax.fori_loop(0, half_rows, rows, 0, unroll=2)
        for step_r in range(3):
            for step_c in range(3):
                pieces = [
                    held[
                        lane,
                        step_r // 2 : step_r // 2 + half_rows,
                        step_r % 2,
                        pl.ds(7 + step_c, half_cols, 2),
                        :,
                    ].reshape(area, 128)
                    for lane in range(lanes)
                ]
                piece = jnp.concatenate(pieces, axis=1).astype(jnp.bfloat16)
                for step_t in range(3):
                    if (frame - step_t) % 2 == 0 and 0 <= frame - step_t < frames:
                        at = (frame - step_t) // 2
                        tap = 9 * step_t + 3 * step_r + step_c
                        patches[at * area : (at + 1) * area, tap * channels : (tap + 1) * channels] = piece
        if frame % 3 == 2 and ticks:
            ticks.pop(0)()

    def tap_grad(tap, _):
        at = pl.multiple_of(tap * channels, channels)
        grads[pl.ds(at, channels), :] = lax.dot_general(
            patches[:, pl.ds(at, channels)],
            cot_ref[...],
            (((0,), (0,)), ((), ())),
            preferred_element_type=jnp.float32,
        )
        return 0

    lax.fori_loop(0, 27, tap_grad, 0)
    for tick in ticks:
        tick()
    for step in range(far_size):
        weight_near(step)

    left = [list(labels) for _ in range(PARTS)]
    copies = [[None] * depth for _ in range(PARTS)]
    piece_rows = grads.shape[0] // (dp_size * tm_size * PARTS)

    def index_of(stride, number, bit):
        return (number // stride) * (2 * stride) + bit * stride + number % stride

    def read(stage, part, index):
        if stage == 0:
            at = (index * PARTS + part) * piece_rows
            if piece_rows % 8 == 0:
                return grads[pl.ds(pl.multiple_of(at, 8), piece_rows), :]
            window = (piece_rows + 14) // 8 * 8
            block = grads[pl.ds(pl.multiple_of(at // 8 * 8, 8), window), :]
            return pltpu.roll(block, (window - at % 8) % window, 0)[:piece_rows]
        return kept[stage - 1][part, index]

    def add(stage, part):
        label = orders[part][stage]
        stride = 2 ** (len(left[part]) - 1 - left[part].index(label))
        number = 2 ** (len(left[part]) - 1)
        copies[part][stage].wait_recv()

        def one(block, _):
            kept[stage][part, block] = read(
                stage, part, index_of(stride, block, bit_of(label))
            ) + receives[stage][part, block].astype(jnp.float32)
            return 0

        lax.fori_loop(0, number, one, 0)
        left[part].remove(label)

    def halve(stage):
        for part in range(PARTS):
            if stage > 0:
                add(stage - 1, part)
            label = orders[part][stage]
            stride = 2 ** (len(left[part]) - 1 - left[part].index(label))
            number = 2 ** (len(left[part]) - 1)

            def pack(block, _):
                sends[stage][part, block] = read(
                    stage, part, index_of(stride, block, 1 - bit_of(label))
                ).astype(jnp.bfloat16)
                return 0

            lax.fori_loop(0, number, pack, 0)
            copies[part][stage] = send(
                sends[stage].at[part], receives[stage].at[part],
                send_sem.at[part, stage], recv_sem.at[part, stage], partner(label),
            )

    halve(0)
    for copy in mate_copies:
        copy.wait_recv()
    own_copy.wait()
    halve(1)
    total = jnp.zeros((count, channels), jnp.float32)
    deep = 9 * channels
    for step in range(3):
        total += jnp.dot(
            patches[:, step * deep : (step + 1) * deep],
            full_weight[step * deep : (step + 1) * deep, :],
            preferred_element_type=jnp.float32,
        )
    out_ref[...] = total.astype(jnp.bfloat16)
    wide[...] = jnp.zeros_like(wide)
    last = jnp.where(tm < tm_size - 1, 1.0, 0.0).astype(jnp.float32)
    for frame in range(frames_out + 1):
        if frame < frames_out:
            piece = cot_ref[frame * area : (frame + 1) * area, :].astype(jnp.float32)
        else:
            piece = next_cot[...].astype(jnp.float32) * last
        wide[frame, 0:half_rows, 0:half_cols, :] = piece.reshape(half_rows, half_cols, channels)
    for dt in range(2):
        for dr in range(2):
            for dc in range(2):
                piece = wide[dt : dt + frames_out, dr : dr + half_rows, dc : dc + half_cols, :]
                views[4 * dt + 2 * dr + dc] = piece.reshape(count, channels).astype(jnp.bfloat16)
    times = (((2, 0), (0, 1)), ((1, 1),))
    spaces = (((1, 0),), ((2, 0), (0, 1)))
    stage = 2
    for part_t in range(2):
        for part_r in range(2):
            for part_c in range(2):
                total = jnp.zeros((count, channels), jnp.float32)
                for step_t, dt in times[part_t]:
                    for step_r, dr in spaces[part_r]:
                        for step_c, dc in spaces[part_c]:
                            tap = 9 * step_t + 3 * step_r + step_c
                            total += lax.dot_general(
                                views[4 * dt + 2 * dr + dc],
                                full_weight[tap * channels : (tap + 1) * channels, :],
                                (((1,), (1,)), ((), ())),
                                preferred_element_type=jnp.float32,
                            )
                total = total.reshape(frames_out, half_rows, half_cols, channels)
                for frame in range(frames_out):
                    for lane in range(lanes):
                        spread[
                            lane, 2 * frame + part_t, :, part_r, pl.ds(part_c, half_cols, 2), :
                        ] = total[frame, :, :, lane * 128 : (lane + 1) * 128]
    halve(stage)

    def back_rows(index, sums):
        frame, row = index // half_rows, index % half_rows
        normed = (clip_ref[frame, row].astype(jnp.float32) - mean) * inv_std
        preact = normed * gain + bias
        sig = 1.0 / (1.0 + jnp.exp(-preact))
        slope = sig * (1.0 + preact * (1.0 - sig))
        hidden_grad = jnp.concatenate([spread[lane, frame, row] for lane in range(lanes)], axis=-1)
        value = hidden_grad * frame_mask(frame) * slope * gain
        for lane in range(lanes):
            spread[lane, frame, row] = value[:, :, lane * 128 : (lane + 1) * 128]
        return sums[0] + fold(value), sums[1] + fold(value * normed)

    finish = exchange(lax.fori_loop(0, frames * half_rows, back_rows, (zero, zero), unroll=2), back_in, 1)
    for stage in range(3, depth):
        halve(stage)
    for part in range(PARTS):
        add(depth - 1, part)
        weight_grad_ref[tm, part] = kept[depth - 1][part, 0]

    tm_bits = [label for label in labels if label[0] == "tm"]
    shares, serial = [], 0
    for label in tm_bits:
        span = 2 ** (label[1] + 1)
        stage_shares = []
        for high in range(tm_size // span):
            block = high * span + tm % span
            stage_shares.append(
                send(weight_grad_ref.at[block], weight_grad_ref.at[block],
                     share_send.at[serial], share_recv.at[serial], partner(label))
            )
            serial += 1
        if label == tm_bits[0]:
            total = finish()
            back_first, back_second = total[0:1] / entries, total[1:2] / entries

            def input_rows(index, _):
                frame, row = index // half_rows, index % half_rows
                normed = (clip_ref[frame, row].astype(jnp.float32) - mean) * inv_std
                value = jnp.concatenate([spread[lane, frame, row] for lane in range(lanes)], axis=-1)
                input_grad_ref[frame, row] = (
                    frame_mask(frame) * inv_std * (value - back_first - normed * back_second)
                ).astype(jnp.bfloat16)
                return 0

            lax.fori_loop(0, frames * half_rows, input_rows, 0, unroll=2)
        for share in stage_shares:
            share.wait_recv()
        shares += stage_shares
    for copy in shares + far_copies + list(near_copies.values()) + mate_copies:
        copy.wait_send()
    for part in range(PARTS):
        for copy in copies[part]:
            copy.wait_send()


def dp_peers(dp, dp_size, near):
    far_at, near_at, far_size = dp // near, dp % near, dp_size // near
    peers = [((far_at + step) % far_size) * near + near_at for step in range(1, far_size)]
    return peers + [far_at * near + (near_at + hop) % near for hop in range(1, near)]


def shards(dp_size, tm_size, clips, frame_counts, weight, gain, bias, cotangent):
    clip_data, cot_block = clips[0], cotangent[0]
    frame_count, row_count, col_count, channels = clip_data.shape
    frames_out, rows_out, cols_out = cot_block.shape[:3]
    area = rows_out * cols_out
    count = frames_out * area
    split = (frame_count, row_count // 2, 2, col_count, channels)
    labels, orders = plan(dp_size, tm_size)
    depth = len(labels)
    rows = dp_size * weight.shape[0]
    piece = rows // (dp_size * tm_size * PARTS)
    halves = [(PARTS, 2 ** (depth - 1 - stage), piece, channels) for stage in range(depth)]
    near = 2 ** ((dp_size.bit_length() - 1) // 2)
    far = dp_size // near
    lanes = channels // 128
    dma = pltpu.SemaphoreType.DMA
    f32, bf16 = jnp.float32, jnp.bfloat16
    output, input_grad, weight_grad = pl.pallas_call(
        functools.partial(block_kernel, labels, orders, dp_size, tm_size, near, channels // GROUPS),
        out_shape=(
            jax.ShapeDtypeStruct((count, channels), bf16),
            jax.ShapeDtypeStruct(split, bf16),
            jax.ShapeDtypeStruct((tm_size, PARTS, piece, channels), f32),
        ),
        in_specs=[SMEM] + [VMEM] * 4,
        out_specs=(VMEM, VMEM, VMEM),
        scratch_shapes=[
            pltpu.VMEM((2,) + split[1:], bf16),
            pltpu.VMEM((area, channels), bf16),
            pltpu.VMEM((rows, channels), bf16),
            pltpu.VMEM((count, rows), bf16),
            pltpu.VMEM((rows, channels), f32),
            pltpu.VMEM((lanes, rows_out + 1, 2, col_count + 8, 128), f32),
            pltpu.VMEM((frames_out + 1, rows_out + 1, 16, channels), f32),
            pltpu.VMEM((8, count, channels), bf16),
            pltpu.VMEM((lanes,) + split[:-1] + (128,), f32),
            pltpu.VMEM((8, channels), f32),
            pltpu.VMEM((tm_size, 8, channels), f32),
            pltpu.VMEM((tm_size, 8, channels), f32),
        ]
        + [pltpu.VMEM(shape, bf16) for shape in halves] * 2
        + [pltpu.VMEM(shape, f32) for shape in halves]
        + [dma((PARTS, depth))] * 2
        + [dma((tm_size,))] * 2
        + [dma((2,))] * 2
        + [dma((2, tm_size))] * 2
        + [dma((far,))] * 2
        + [dma((far, near))] * 4
        + [dma(())],
        compiler_params=pltpu.CompilerParams(
            collective_id=0, has_side_effects=True, vmem_limit_bytes=56 * 2**20
        ),
    )(frame_counts, jnp.stack([gain, bias]), clip_data.reshape(split), cot_block.reshape(count, channels), weight)
    return (
        output.reshape(cot_block.shape)[None],
        input_grad.reshape(clip_data.shape)[None],
        weight_grad.reshape(weight.shape),
    )


def solution(mesh):
    placed = (
        P("dp", "tm", None, None, None),
        P("dp"),
        P("dp", None),
        P(),
        P(),
        P("dp", "tm", None, None, None),
    )
    return jax.shard_map(
        functools.partial(shards, mesh.shape["dp"], mesh.shape["tm"]),
        mesh=mesh,
        in_specs=placed,
        out_specs=(P("dp", "tm", None, None, None), P("dp", "tm", None, None, None), P("dp", None)),
        check_vma=False,
    )
```

```python
import functools

import jax
import jax.numpy as jnp
from jax import lax
from jax.experimental import pallas as pl
from jax.experimental.pallas import tpu as pltpu
from jax.sharding import PartitionSpec as P

GROUPS = 32
EPS = 1e-06
PARTS = 3
MESH = pl.DeviceIdType.MESH
VMEM = pl.BlockSpec(memory_space=pltpu.VMEM)
SMEM = pl.BlockSpec(memory_space=pltpu.SMEM)


def plan(dp_size, tm_size):
    dp_bits = [("dp", k) for k in range(dp_size.bit_length() - 1)]
    tm_bits = [("tm", k) for k in range(tm_size.bit_length() - 1)]
    cut = len(dp_bits) // 2
    ways = [tm_bits[1:], dp_bits[:cut], dp_bits[cut:]]
    orders = []
    for part in range(PARTS):
        turned = ways[part:] + ways[:part]
        orders.append(tm_bits[:1] + turned[0] + turned[1] + turned[2])
    return dp_bits[::-1] + tm_bits[::-1], orders


def lane_group_sum(value, width):
    channels = value.shape[-1]
    lane = lax.broadcasted_iota(jnp.int32, value.shape, value.ndim - 1)
    step = 1
    while step < width:
        above = pltpu.roll(value, channels - step, value.ndim - 1)
        below = pltpu.roll(value, step, value.ndim - 1)
        value = value + jnp.where((lane // step) % 2 == 0, above, below)
        step *= 2
    return value


def block_kernel(
    labels, orders, dp_size, tm_size, near, width_g,
    valid_ref, params_ref, clip_ref, cot_ref, weight_ref,
    out_ref, input_grad_ref, weight_grad_ref,
    earlier, next_cot, full_weight, patches, grads, held, wide, views, spread, shared, sums_in, back_in,
    *scratch,
):
    frames, half_rows, _, cols, channels = clip_ref.shape
    frames_out, half_cols, lanes = frames // 2, cols // 2, channels // 128
    area = half_rows * half_cols
    count = frames_out * area
    depth = len(labels)
    sends, receives, kept = (scratch[i * depth : (i + 1) * depth] for i in range(3))
    (send_sem, recv_sem, share_send, share_recv, ring_send, ring_recv, sum_send, sum_recv,
     far_send, far_recv, near_send, near_recv, mate_send, mate_recv, cross_send, cross_recv, own_sem) = scratch[3 * depth :]
    dp, tm = lax.axis_index("dp"), lax.axis_index("tm")
    place = {"dp": dp, "tm": tm}
    far_size = dp_size // near
    far_at, near_at = dp // near, dp % near
    core = tm % 2
    mate = {"tm": tm + 1 - 2 * core}

    def bit_of(label):
        return (place[label[0]] // 2 ** label[1]) % 2

    def partner(label):
        return {label[0]: place[label[0]] + (1 - 2 * bit_of(label)) * 2 ** label[1]}

    def send(source, target, sem_out, sem_in, device):
        copy = pltpu.make_async_remote_copy(
            src_ref=source, dst_ref=target, send_sem=sem_out, recv_sem=sem_in,
            device_id=device, device_id_type=MESH,
        )
        copy.start()
        return copy

    barrier = pltpu.get_barrier_semaphore()
    greeted = [{"tm": (tm + step) % tm_size} for step in range(1, tm_size)]
    greeted += [{"dp": dp_index} for dp_index in dp_peers(dp, dp_size, near)]
    for device in greeted:
        pl.semaphore_signal(barrier, inc=1, device_id=device, device_id_type=MESH)
    pl.semaphore_wait(barrier, len(greeted))

    ring = [
        send(clip_ref.at[frames - 2 : frames], earlier, ring_send.at[0], ring_recv.at[0], {"tm": (tm + 1) % tm_size}),
        send(cot_ref.at[0:area], next_cot, ring_send.at[1], ring_recv.at[1], {"tm": (tm + tm_size - 1) % tm_size}),
    ]

    rows_w = weight_ref.shape[0]
    half_lane = pl.ds(pl.multiple_of(core * 128, 128), 128)

    crossed = tm_size == 4 and rows_w % 48 == 0
    rows_x = rows_w // 3 if crossed else 0
    span_w = rows_w - rows_x
    across = (tm // 2) % 2 if crossed else 0
    cross_mate = {"tm": (tm + 2) % tm_size}
    span_at = across * rows_x

    def rows_of(index, start, size):
        return full_weight.at[pl.ds(pl.multiple_of(index * rows_w + start, 8), size), half_lane]

    def block_at(index):
        return rows_of(index, span_at, span_w)

    own_copy = pltpu.make_async_copy(
        weight_ref, full_weight.at[pl.ds(pl.multiple_of(dp * rows_w, 8), rows_w), :], own_sem
    )
    own_copy.start()
    own_half = weight_ref.at[pl.ds(pl.multiple_of(span_at, 8), span_w), half_lane]
    far_copies = [
        send(own_half, block_at(dp), far_send.at[step], far_recv.at[step],
             {"dp": ((far_at + step) % far_size) * near + near_at})
        for step in range(1, far_size)
    ]
    near_copies, mate_copies, cross_copies = {}, [], []

    def send_near(step, source, index):
        for hop in range(1, near):
            near_copies[step, hop] = send(
                source, block_at(index), near_send.at[step, hop], near_recv.at[step, hop],
                {"dp": far_at * near + (near_at + hop) % near},
            )

    def send_mate(step, hop, index):
        if crossed:
            cross = rows_of(index, across * (span_w), rows_x)
            copy = send(cross, cross, cross_send.at[step, hop], cross_recv.at[step, hop], cross_mate)
            cross_copies.append((copy, step, hop, index))
        mate_copies.append(
            send(block_at(index), block_at(index), mate_send.at[0, step, hop], mate_recv.at[0, step, hop], mate)
        )

    def weight_cross():
        for copy, step, hop, index in cross_copies:
            copy.wait_recv()
            rest = rows_of(index, (1 - across) * span_w, rows_x)
            mate_copies.append(
                send(rest, rest, mate_send.at[1, step, hop], mate_recv.at[1, step, hop], mate)
            )

    send_near(0, own_half, dp)

    def weight_far(step):
        far_copies[step - 1].wait_recv()
        index = ((far_at + far_size - step) % far_size) * near + near_at
        send_near(step, block_at(index), index)
        send_mate(step, 0, index)

    def weight_near(step):
        for hop in range(1, near):
            near_copies[step, hop].wait_recv()
            index = ((far_at + far_size - step) % far_size) * near + (near_at + near - hop) % near
            send_mate(step, hop, index)

    first = tm * frames
    valid = valid_ref[0]
    gain, bias = params_ref[0:1, :], params_ref[1:2, :]
    entries = jnp.full((1, channels), valid.astype(jnp.float32)) * float(2 * half_rows * cols * width_g)
    zero = jnp.zeros((8, channels), jnp.float32)

    def fold(value):
        return jnp.sum(value.reshape(-1, 8, channels), axis=0)

    def frame_mask(frame):
        slot = first + frame
        return jnp.where((slot >= 0) & (slot < valid), 1.0, 0.0).astype(jnp.float32)

    def moment_rows(index, sums):
        frame, row = index // half_rows, index % half_rows
        values = clip_ref[frame, row].astype(jnp.float32)
        masked = values * frame_mask(frame)
        return sums[0] + fold(masked), sums[1] + fold(masked * values)

    def exchange(sums, buffer, sems):
        pair = [jnp.sum(value, axis=0, keepdims=True) for value in sums]
        buffer[tm] = jnp.concatenate(pair + [jnp.zeros((6, channels), jnp.float32)], axis=0)
        copies = [
            send(buffer.at[tm], buffer.at[tm], sum_send.at[sems, step], sum_recv.at[sems, step],
                 {"tm": (tm + step) % tm_size})
            for step in range(1, tm_size)
        ]

        def finish():
            for copy in copies:
                copy.wait()
            total = buffer[0]
            for index in range(1, tm_size):
                total = total + buffer[index]
            return lane_group_sum(total, width_g)

        return finish

    finish = exchange(lax.fori_loop(0, frames * half_rows, moment_rows, (zero, zero), unroll=4), sums_in, 0)
    held[...] = jnp.zeros_like(held)
    total = finish()
    mean = total[0:1] / entries
    inv_std = lax.rsqrt(total[1:2] / entries - mean * mean + EPS)
    for copy in ring:
        copy.wait()

    ticks = [functools.partial(weight_far, step) for step in range(1, far_size)]
    for frame in range(frames + 1):
        source = earlier.at[frame] if frame < 2 else clip_ref.at[frame - 2]
        mask = frame_mask(frame - 2)

        def rows(index, _):
            values = source[index].astype(jnp.float32)
            preact = (values - mean) * inv_std * gain + bias
            hidden = preact / (1.0 + jnp.exp(-preact)) * mask
            for lane in range(lanes):
                part = hidden[:, :, lane * 128 : (lane + 1) * 128]
                held[lane, index, 1, 8 : 8 + cols, :] = part[0]
                held[lane, index + 1, 0, 8 : 8 + cols, :] = part[1]
            return 0

        lax.fori_loop(0, half_rows, rows, 0, unroll=4)
        for step_r in range(3):
            for step_c in range(3):
                pieces = [
                    held[
                        lane,
                        step_r // 2 : step_r // 2 + half_rows,
                        step_r % 2,
                        pl.ds(7 + step_c, half_cols, 2),
                        :,
                    ].reshape(area, 128)
                    for lane in range(lanes)
                ]
                piece = jnp.concatenate(pieces, axis=1).astype(jnp.bfloat16)
                for step_t in range(3):
                    if (frame - step_t) % 2 == 0 and 0 <= frame - step_t < frames:
                        at = (frame - step_t) // 2
                        tap = 9 * step_t + 3 * step_r + step_c
                        patches[at * area : (at + 1) * area, tap * channels : (tap + 1) * channels] = piece
        if frame % 3 == 2 and ticks:
            ticks.pop(0)()

    def tap_grad(tap, _):
        at = pl.multiple_of(tap * channels, channels)
        grads[pl.ds(at, channels), :] = lax.dot_general(
            patches[:, pl.ds(at, channels)],
            cot_ref[...],
            (((0,), (0,)), ((), ())),
            preferred_element_type=jnp.float32,
        )
        return 0

    for tick in ticks:
        tick()
    weight_near(0)
    lax.fori_loop(0, 27, tap_grad, 0)

    left = [list(labels) for _ in range(PARTS)]
    copies = [[None] * depth for _ in range(PARTS)]
    piece_rows = grads.shape[0] // (dp_size * tm_size * PARTS)

    def index_of(stride, number, bit):
        return (number // stride) * (2 * stride) + bit * stride + number % stride

    def read(stage, part, index):
        if stage == 0:
            at = (index * PARTS + part) * piece_rows
            if piece_rows % 8 == 0:
                return grads[pl.ds(pl.multiple_of(at, 8), piece_rows), :]
            window = (piece_rows + 14) // 8 * 8
            block = grads[pl.ds(pl.multiple_of(at // 8 * 8, 8), window), :]
            return pltpu.roll(block, (window - at % 8) % window, 0)[:piece_rows]
        return kept[stage - 1][part, index]

    def add(stage, part):
        label = orders[part][stage]
        stride = 2 ** (len(left[part]) - 1 - left[part].index(label))
        number = 2 ** (len(left[part]) - 1)
        copies[part][stage].wait_recv()

        def one(block, _):
            kept[stage][part, block] = read(
                stage, part, index_of(stride, block, bit_of(label))
            ) + receives[stage][part, block].astype(jnp.float32)
            return 0

        lax.fori_loop(0, number, one, 0)
        left[part].remove(label)

    def halve(stage):
        for part in range(PARTS):
            if stage > 0:
                add(stage - 1, part)
            label = orders[part][stage]
            stride = 2 ** (len(left[part]) - 1 - left[part].index(label))
            number = 2 ** (len(left[part]) - 1)

            def pack(block, _):
                sends[stage][part, block] = read(
                    stage, part, index_of(stride, block, 1 - bit_of(label))
                ).astype(jnp.bfloat16)
                return 0

            lax.fori_loop(0, number, pack, 0)
            copies[part][stage] = send(
                sends[stage].at[part], receives[stage].at[part],
                send_sem.at[part, stage], recv_sem.at[part, stage], partner(label),
            )

    halve(0)
    for step in range(1, far_size):
        weight_near(step)
    halve(1)
    weight_cross()
    for copy in mate_copies:
        copy.wait_recv()
    own_copy.wait()
    total = jnp.zeros((count, channels), jnp.float32)
    deep = 9 * channels
    for step in range(3):
        total += jnp.dot(
            patches[:, step * deep : (step + 1) * deep],
            full_weight[step * deep : (step + 1) * deep, :],
            preferred_element_type=jnp.float32,
        )
    out_ref[...] = total.astype(jnp.bfloat16)
    wide[...] = jnp.zeros_like(wide)
    last = jnp.where(tm < tm_size - 1, 1.0, 0.0).astype(jnp.float32)
    for frame in range(frames_out + 1):
        if frame < frames_out:
            piece = cot_ref[frame * area : (frame + 1) * area, :].astype(jnp.float32)
        else:
            piece = next_cot[...].astype(jnp.float32) * last
        wide[frame, 0:half_rows, 0:half_cols, :] = piece.reshape(half_rows, half_cols, channels)
    for dt in range(2):
        for dr in range(2):
            for dc in range(2):
                piece = wide[dt : dt + frames_out, dr : dr + half_rows, dc : dc + half_cols, :]
                views[4 * dt + 2 * dr + dc] = piece.reshape(count, channels).astype(jnp.bfloat16)
    times = (((2, 0), (0, 1)), ((1, 1),))
    spaces = (((1, 0),), ((2, 0), (0, 1)))
    stage = 2
    for part_t in range(2):
        for part_r in range(2):
            for part_c in range(2):
                total = jnp.zeros((count, channels), jnp.float32)
                for step_t, dt in times[part_t]:
                    for step_r, dr in spaces[part_r]:
                        for step_c, dc in spaces[part_c]:
                            tap = 9 * step_t + 3 * step_r + step_c
                            total += lax.dot_general(
                                views[4 * dt + 2 * dr + dc],
                                full_weight[tap * channels : (tap + 1) * channels, :],
                                (((1,), (1,)), ((), ())),
                                preferred_element_type=jnp.float32,
                            )
                total = total.reshape(frames_out, half_rows, half_cols, channels)
                for frame in range(frames_out):
                    for lane in range(lanes):
                        spread[
                            lane, 2 * frame + part_t, :, part_r, pl.ds(part_c, half_cols, 2), :
                        ] = total[frame, :, :, lane * 128 : (lane + 1) * 128]
    halve(stage)

    def back_rows(index, sums):
        frame, row = index // half_rows, index % half_rows
        normed = (clip_ref[frame, row].astype(jnp.float32) - mean) * inv_std
        preact = normed * gain + bias
        sig = 1.0 / (1.0 + jnp.exp(-preact))
        slope = sig * (1.0 + preact * (1.0 - sig))
        hidden_grad = jnp.concatenate([spread[lane, frame, row] for lane in range(lanes)], axis=-1)
        value = hidden_grad * frame_mask(frame) * slope * gain
        for lane in range(lanes):
            spread[lane, frame, row] = value[:, :, lane * 128 : (lane + 1) * 128]
        return sums[0] + fold(value), sums[1] + fold(value * normed)

    finish = exchange(lax.fori_loop(0, frames * half_rows, back_rows, (zero, zero), unroll=4), back_in, 1)
    for stage in range(3, depth):
        halve(stage)
    for part in range(PARTS):
        add(depth - 1, part)
        shared[tm, part] = kept[depth - 1][part, 0].astype(jnp.bfloat16)

    tm_bits = [label for label in labels if label[0] == "tm"]
    shares, serial = [], 0
    for label in tm_bits:
        span = 2 ** (label[1] + 1)
        stage_shares = []
        for high in range(tm_size // span):
            block = high * span + tm % span
            stage_shares.append(
                send(shared.at[block], shared.at[block],
                     share_send.at[serial], share_recv.at[serial], partner(label))
            )
            serial += 1
        if label == tm_bits[0]:
            total = finish()
            back_first, back_second = total[0:1] / entries, total[1:2] / entries

            def input_rows(index, _):
                frame, row = index // half_rows, index % half_rows
                normed = (clip_ref[frame, row].astype(jnp.float32) - mean) * inv_std
                value = jnp.concatenate([spread[lane, frame, row] for lane in range(lanes)], axis=-1)
                input_grad_ref[frame, row] = (
                    frame_mask(frame) * inv_std * (value - back_first - normed * back_second)
                ).astype(jnp.bfloat16)
                return 0

            lax.fori_loop(0, frames * half_rows, input_rows, 0, unroll=4)
        for share in stage_shares:
            share.wait_recv()
        shares += stage_shares
    for block in range(tm_size):
        weight_grad_ref[block] = shared[block].astype(jnp.float32)
    for copy in shares + far_copies + list(near_copies.values()) + mate_copies + [item[0] for item in cross_copies]:
        copy.wait_send()
    for part in range(PARTS):
        for copy in copies[part]:
            copy.wait_send()


def dp_peers(dp, dp_size, near):
    far_at, near_at, far_size = dp // near, dp % near, dp_size // near
    peers = [((far_at + step) % far_size) * near + near_at for step in range(1, far_size)]
    return peers + [far_at * near + (near_at + hop) % near for hop in range(1, near)]


def shards(dp_size, tm_size, clips, frame_counts, weight, gain, bias, cotangent):
    clip_data, cot_block = clips[0], cotangent[0]
    frame_count, row_count, col_count, channels = clip_data.shape
    frames_out, rows_out, cols_out = cot_block.shape[:3]
    area = rows_out * cols_out
    count = frames_out * area
    split = (frame_count, row_count // 2, 2, col_count, channels)
    labels, orders = plan(dp_size, tm_size)
    depth = len(labels)
    rows = dp_size * weight.shape[0]
    piece = rows // (dp_size * tm_size * PARTS)
    halves = [(PARTS, 2 ** (depth - 1 - stage), piece, channels) for stage in range(depth)]
    near = 2 ** ((dp_size.bit_length() - 1) // 2)
    far = dp_size // near
    lanes = channels // 128
    dma = pltpu.SemaphoreType.DMA
    f32, bf16 = jnp.float32, jnp.bfloat16
    output, input_grad, weight_grad = pl.pallas_call(
        functools.partial(block_kernel, labels, orders, dp_size, tm_size, near, channels // GROUPS),
        out_shape=(
            jax.ShapeDtypeStruct((count, channels), bf16),
            jax.ShapeDtypeStruct(split, bf16),
            jax.ShapeDtypeStruct((tm_size, PARTS, piece, channels), f32),
        ),
        in_specs=[SMEM] + [VMEM] * 4,
        out_specs=(VMEM, VMEM, VMEM),
        scratch_shapes=[
            pltpu.VMEM((2,) + split[1:], bf16),
            pltpu.VMEM((area, channels), bf16),
            pltpu.VMEM((rows, channels), bf16),
            pltpu.VMEM((count, rows), bf16),
            pltpu.VMEM((rows, channels), f32),
            pltpu.VMEM((lanes, rows_out + 1, 2, col_count + 8, 128), f32),
            pltpu.VMEM((frames_out + 1, rows_out + 1, 16, channels), f32),
            pltpu.VMEM((8, count, channels), bf16),
            pltpu.VMEM((lanes,) + split[:-1] + (128,), f32),
            pltpu.VMEM((tm_size, PARTS, piece, channels), bf16),
            pltpu.VMEM((tm_size, 8, channels), f32),
            pltpu.VMEM((tm_size, 8, channels), f32),
        ]
        + [pltpu.VMEM(shape, bf16) for shape in halves] * 2
        + [pltpu.VMEM(shape, f32) for shape in halves]
        + [dma((PARTS, depth))] * 2
        + [dma((tm_size,))] * 2
        + [dma((2,))] * 2
        + [dma((2, tm_size))] * 2
        + [dma((far,))] * 2
        + [dma((far, near))] * 2
        + [dma((2, far, near))] * 2
        + [dma((far, near))] * 2
        + [dma(())],
        compiler_params=pltpu.CompilerParams(
            collective_id=0, has_side_effects=True, vmem_limit_bytes=56 * 2**20
        ),
    )(frame_counts, jnp.stack([gain, bias]), clip_data.reshape(split), cot_block.reshape(count, channels), weight)
    return (
        output.reshape(cot_block.shape)[None],
        input_grad.reshape(clip_data.shape)[None],
        weight_grad.reshape(weight.shape),
    )


def solution(mesh):
    placed = (
        P("dp", "tm", None, None, None),
        P("dp"),
        P("dp", None),
        P(),
        P(),
        P("dp", "tm", None, None, None),
    )
    return jax.shard_map(
        functools.partial(shards, mesh.shape["dp"], mesh.shape["tm"]),
        mesh=mesh,
        in_specs=placed,
        out_specs=(P("dp", "tm", None, None, None), P("dp", "tm", None, None, None), P("dp", None)),
        check_vma=False,
    )
```
